32 devices in a mesh: shard: 2 (over core), rep: 16 (over z, y, x).
Axes of the slice: x: 2, y: 2, z: 4, core: 2. Of those that a mesh axis runs over, the one named last changes fastest.
Arguments:
- block_input: float32 [96, 14, 14, 512], P(('shard', 'rep')), may hold values from -6 to 6
- ln1_gain: bfloat16 [512], P('shard'), may hold values from 0.5 to 1.5
- ln1_bias: bfloat16 [512], P('shard'), may hold values from -2 to 2
- qkv_weight: bfloat16 [512, 1536], P('shard'), may hold values from -0.25 to 0.25
- qv_bias: bfloat16 [2, 512], P(None, 'shard'), may hold values from -2 to 2
- bias_table: bfloat16 [169, 16], P(None, 'shard'), may hold values from -4 to 4
- proj_weight: bfloat16 [512, 512], P('shard'), may hold values from -0.5 to 0.5
- proj_bias: bfloat16 [512], P('shard'), may hold values from -2 to 2
- ln2_gain: bfloat16 [512], P('shard'), may hold values from 0.5 to 1.5
- ln2_bias: bfloat16 [512], P('shard'), may hold values from -2 to 2
- fc1_weight: bfloat16 [512, 2048], P('shard'), may hold values from -0.25 to 0.25
- fc1_bias: bfloat16 [2048], P('shard'), may hold values from -2 to 2
- fc2_weight: bfloat16 [2048, 512], P('shard'), may hold values from -0.125 to 0.125
- fc2_bias: bfloat16 [512], P('shard'), may hold values from -2 to 2
- region_ids: int32 [14, 14], replicated, may hold values from 0 to 3
- rel_index: int32 [49, 49], replicated, may hold values from 0 to 168
- cotangent: float32 [96, 14, 14, 512], P(('shard', 'rep')), may hold values from -6 to 6
Outputs:
- block_output: float32 [96, 14, 14, 512], P(('shard', 'rep'))
- input_gradient_total: float32 [96, 14, 14, 512], P(('shard', 'rep'))
- grad_ln1_gain: float32 [512], P('shard')
- grad_ln1_bias: float32 [512], P('shard')
- grad_qkv_weight: float32 [512, 1536], P('shard')
- grad_qv_bias: float32 [2, 512], P(None, 'shard')
- grad_bias_table: float32 [169, 16], P(None, 'shard')
- grad_proj_weight: float32 [512, 512], P('shard')
- grad_proj_bias: float32 [512], P('shard')
- grad_ln2_gain: float32 [512], P('shard')
- grad_ln2_bias: float32 [512], P('shard')
- grad_fc1_weight: float32 [512, 2048], P('shard')
- grad_fc1_bias: float32 [2048], P('shard')
- grad_fc2_weight: float32 [2048, 512], P('shard')
- grad_fc2_bias: float32 [512], P('shard')
The draws below stay inside these ranges and needn't reach their ends.
All inputs are finite; a program needn't handle non-finite values.
Results may differ from the reference program's by a relative error of at most 0.017.
Values may be sent and summed in bfloat16 or wider, within the bound.
No kernel may reach another device: no remote copies, remote signals or barrier semaphores. Data moves between devices by JAX's collectives and lax.ppermute only.
A program may use at most 128 MiB of HBM per device.

```python
import jax
import jax.numpy as jnp
from jax import lax

C = 512
HEADS = 16
HIDDEN_SIZE = 2048
SIDE = 14
WIN = 7
SHIFT = 3
IMG_DEV = 3
TABLE = 169
IMAGES = 96
N_SHARD = 2


def touch_ends(values, key, smallest, top_value):
    longest = values.shape.index(max(values.shape))
    spots = []
    for shift in (0, 1):
        where = [jax.random.randint(jax.random.fold_in(key, axis), (), 0, length) for axis, length in enumerate(values.shape)]
        where[longest] = (where[longest] + shift) % values.shape[longest]
        spots.append(tuple(where))
    return values.at[spots[0]].set(smallest).at[spots[1]].set(top_value)


def level_of(own_key, extent, split, low, high):
    def one(dim, blocks):
        steps = jax.random.uniform(jax.random.fold_in(jax.random.fold_in(own_key, 6), dim), (blocks,), jnp.float32, low / len(split), high / len(split))
        return jnp.repeat(jnp.exp(steps), extent[dim] // blocks).reshape((-1,) + (1,) * (len(extent) - dim - 1))

    level = one(*split[0])
    for cut in split[1:]:
        level = level * one(*cut)
    return level


def gaussian(rng, extent, scale, most, split=(), kind=jnp.bfloat16):
    drawn = scale * jax.random.normal(rng, extent, jnp.float32)
    if split:
        drawn = drawn * level_of(rng, extent, split, -0.22, 0.18)
    return jnp.clip(drawn, -most, most).astype(kind)


def setup_inputs(seed: int = 0) -> dict:
    key_of = jax.random.split(jax.random.key(seed), 18)
    block_input = gaussian(key_of[0], (IMAGES, SIDE, SIDE, C), 1.0, 6.0, ((0, 32),), jnp.float32)
    ln1_gain = jnp.clip(1.0 + 0.1 * jax.random.normal(key_of[1], (C,), jnp.float32), 0.5, 1.5).astype(jnp.bfloat16)
    ln1_bias = gaussian(key_of[2], (C,), 0.3, 2.0, ((0, 2),))
    qkv_weight = gaussian(key_of[3], (C, 3 * C), C ** -0.5, 0.25, ((0, 2),))
    qv_bias = gaussian(key_of[4], (2, C), 0.3, 2.0, ((1, 2),))
    bias_table = gaussian(key_of[5], (TABLE, HEADS), 1.0, 4.0, ((1, 2),))
    proj_weight = gaussian(key_of[6], (C, C), (C // 4) ** -0.5, 0.5, ((0, 2),))
    proj_bias = gaussian(key_of[7], (C,), 0.3, 2.0, ((0, 2),))
    ln2_gain = jnp.clip(1.0 + 0.1 * jax.random.normal(key_of[8], (C,), jnp.float32), 0.5, 1.5).astype(jnp.bfloat16)
    ln2_bias = gaussian(key_of[9], (C,), 0.3, 2.0, ((0, 2),))
    fc1_weight = gaussian(key_of[10], (C, HIDDEN_SIZE), C ** -0.5, 0.25, ((0, 2),))
    fc1_bias = gaussian(key_of[11], (HIDDEN_SIZE,), 0.3, 2.0, ((0, 2),))
    fc2_weight = gaussian(key_of[12], (HIDDEN_SIZE, C), HIDDEN_SIZE ** -0.5, 0.125, ((0, 2),))
    fc2_bias = gaussian(key_of[13], (C,), 0.3, 2.0, ((0, 2),))
    region_ids = touch_ends(jax.random.randint(key_of[14], (SIDE, SIDE), 0, 4), jax.random.fold_in(key_of[14], 1), 0, 3).astype(jnp.int32)
    rel_index = touch_ends(jax.random.randint(key_of[15], (WIN * WIN, WIN * WIN), 0, TABLE), jax.random.fold_in(key_of[15], 1), 0, TABLE - 1).astype(jnp.int32)
    cotangent = gaussian(key_of[16], (IMAGES, SIDE, SIDE, C), 1.0, 6.0, ((0, 32),), jnp.float32)
    return dict(block_input=block_input, ln1_gain=ln1_gain, ln1_bias=ln1_bias, qkv_weight=qkv_weight, qv_bias=qv_bias, bias_table=bias_table, proj_weight=proj_weight, proj_bias=proj_bias, ln2_gain=ln2_gain, ln2_bias=ln2_bias, fc1_weight=fc1_weight, fc1_bias=fc1_bias, fc2_weight=fc2_weight, fc2_bias=fc2_bias, region_ids=region_ids, rel_index=rel_index, cotangent=cotangent)


EPS = 1e-05
MASKED = -100.0
INV_ROOT_TWO = 0.7071067811865476
INV_ROOT_TWO_PI = 0.3989422804014327

def to_windows(t):
    count = t.shape[0]
    window_width = t.shape[-1]
    grid = SIDE // WIN
    t = jnp.roll(t, (-SHIFT, -SHIFT), (1, 2))
    t = t.reshape(count, grid, WIN, grid, WIN, window_width).transpose(0, 1, 3, 2, 4, 5)
    return t.reshape(count * grid * grid, WIN * WIN, window_width)

def from_windows(t, count):
    grid = SIDE // WIN
    window_width = t.shape[-1]
    t = t.reshape(count, grid, grid, WIN, WIN, window_width).transpose(0, 1, 3, 2, 4, 5)
    t = t.reshape(count, SIDE, SIDE, window_width)
    return jnp.roll(t, (SHIFT, SHIFT), (1, 2))

def mask_table(region_ids):
    grid = SIDE // WIN
    labels = region_ids.reshape(grid, WIN, grid, WIN).transpose(0, 2, 1, 3).reshape(grid * grid, WIN * WIN)
    same = labels[:, :, None] == labels[:, None, :]
    return jnp.where(same, jnp.float32(0.0), jnp.float32(MASKED)).astype(jnp.float32)

def norm_forward(v, gain, bias):
    mean_v = lax.optimization_barrier(jnp.mean(v, -1, keepdims=True))
    centered = v - mean_v
    var_v = lax.optimization_barrier(jnp.mean(centered * centered, -1, keepdims=True))
    inv_std = lax.rsqrt(var_v + EPS)
    normed = centered * inv_std
    return (normed, inv_std, normed * gain.astype(jnp.float32) + bias.astype(jnp.float32))

def norm_backward(grad, normed, inv_std, gain):
    window_width = grad.shape[-1]
    dnormed = grad * gain.astype(jnp.float32)
    dv = inv_std * (dnormed - lax.optimization_barrier(jnp.mean(dnormed, -1, keepdims=True)) - normed * lax.optimization_barrier(jnp.mean(dnormed * normed, -1, keepdims=True)))
    grad_gain = lax.optimization_barrier(jnp.sum((grad * normed).reshape(-1, window_width), 0))
    grad_bias = lax.optimization_barrier(jnp.sum(grad.reshape(-1, window_width), 0))
    return (dv, grad_gain, grad_bias)

def gelu_slope(u):
    return 0.5 * (1.0 + lax.erf(u * INV_ROOT_TWO)) + u * jnp.exp(-0.5 * u * u) * INV_ROOT_TWO_PI

def attn_scores(query, keys, extra, count):
    scores = jnp.einsum('bihd,bjhd->bhij', query.astype(jnp.float32), keys.astype(jnp.float32))
    shape = scores.shape
    grid = SIDE // WIN
    scores = scores.reshape((count, grid * grid) + shape[1:]) + extra[None]
    return scores.reshape(shape)

def block_pass(xb, dyb, params, rel_index, region_ids):
    g1, b1, wqkv, bqv, table, wp, bp, g2, b2, w1, bf1, w2, bf2 = params
    f32 = jnp.float32
    bf = jnp.bfloat16
    count = xb.shape[0]
    window_width = xb.shape[-1]
    heads = table.shape[1]
    hdim = window_width // heads
    seq = WIN * WIN
    scale = hdim ** (-0.5)
    xn1, inv1, h1 = norm_forward(xb, g1, b1)
    hw = to_windows(h1.astype(bf))
    nwin = hw.shape[0]
    hw_rows = hw.reshape(-1, window_width)
    qkv = jnp.dot(hw_rows, wqkv, preferred_element_type=f32).reshape(nwin, seq, 3 * window_width)
    query = ((qkv[..., :window_width] + bqv[0].astype(f32)) * scale).astype(bf).reshape(nwin, seq, heads, hdim)
    keys = qkv[..., window_width:2 * window_width].astype(bf).reshape(nwin, seq, heads, hdim)
    values = (qkv[..., 2 * window_width:] + bqv[1].astype(f32)).astype(bf).reshape(nwin, seq, heads, hdim)
    rel = table.astype(f32)[rel_index].transpose(2, 0, 1)
    extra = mask_table(region_ids)[:, None] + rel[None]
    scores = attn_scores(query, keys, extra, count)
    lse = jnp.log(lax.optimization_barrier(jnp.sum(jnp.exp(scores), -1, keepdims=True)))
    probs = jnp.exp(scores - lse)
    probs_b = probs.astype(bf)
    attn_out = jnp.einsum('bhij,bjhd->bihd', probs_b.astype(f32), values.astype(f32))
    attn_out = attn_out.reshape(nwin, seq, window_width).astype(bf)
    attn_rows = attn_out.reshape(-1, window_width)
    branch = (jnp.dot(attn_rows, wp, preferred_element_type=f32) + bp.astype(f32)).reshape(nwin, seq, window_width)
    x1 = xb + from_windows(branch, count)
    xn2, inv2, h2f = norm_forward(x1, g2, b2)
    h2 = h2f.astype(bf).reshape(-1, window_width)
    pre = jnp.dot(h2, w1, preferred_element_type=f32) + bf1.astype(f32)
    act = jax.nn.gelu(pre, approximate=False).astype(bf)
    final_output = x1 + (jnp.dot(act, w2, preferred_element_type=f32) + bf2.astype(f32)).reshape(xb.shape)
    dy_rows = dyb.reshape(-1, window_width)
    dyh = dy_rows.astype(bf)
    output_weight_gradient = jnp.dot(act.T, dyh, preferred_element_type=f32)
    output_bias_gradient = lax.optimization_barrier(jnp.sum(dy_rows, 0))
    dpre = jnp.dot(dyh, w2.T, preferred_element_type=f32) * gelu_slope(pre)
    dpre_b = dpre.astype(bf)
    hidden_weight_gradient = jnp.dot(h2.T, dpre_b, preferred_element_type=f32)
    hidden_bias_gradient = lax.optimization_barrier(jnp.sum(dpre, 0))
    dh2 = jnp.dot(dpre_b, w1.T, preferred_element_type=f32).reshape(xb.shape)
    dx1n, second_gain_gradient, second_norm_bias_gradient = norm_backward(dh2, xn2, inv2, g2)
    input_gradient_first = dyb + dx1n
    dwin = to_windows(input_gradient_first).astype(bf).reshape(-1, window_width)
    projection_weight_gradient = jnp.dot(attn_rows.T, dwin, preferred_element_type=f32)
    projection_bias_gradient = lax.optimization_barrier(jnp.sum(input_gradient_first.reshape(-1, window_width), 0))
    dout = jnp.dot(dwin, wp.T, preferred_element_type=f32).astype(bf).reshape(nwin, seq, heads, hdim)
    scores2 = attn_scores(query, keys, extra, count)
    probs2 = jnp.exp(scores2 - lse)
    probs2_b = probs2.astype(bf)
    dvals = jnp.einsum('bhij,bihd->bjhd', probs2_b.astype(f32), dout.astype(f32))
    dprobs = jnp.einsum('bihd,bjhd->bhij', dout.astype(f32), values.astype(f32))
    dscores = probs2 * (dprobs - lax.optimization_barrier(jnp.sum(probs2 * dprobs, -1, keepdims=True)))
    dbias = lax.optimization_barrier(jnp.sum(dscores, 0)).reshape(heads, seq * seq)
    bias_table_gradient = jnp.zeros((TABLE, heads), f32).at[rel_index.reshape(-1)].add(dbias.T)
    dscores_b = dscores.astype(bf).astype(f32)
    dquery = jnp.einsum('bhij,bjhd->bihd', dscores_b, keys.astype(f32)) * scale
    dkeys = jnp.einsum('bhij,bihd->bjhd', dscores_b, query.astype(f32))
    dquery = dquery.reshape(-1, window_width)
    dvals = dvals.reshape(-1, window_width)
    query_value_bias_gradient = jnp.stack([lax.optimization_barrier(jnp.sum(dquery, 0)), lax.optimization_barrier(jnp.sum(dvals, 0))])
    dqkv = jnp.concatenate([dquery, dkeys.reshape(-1, window_width), dvals], -1).astype(bf)
    query_key_value_gradient = jnp.dot(hw_rows.T, dqkv, preferred_element_type=f32)
    dh1 = from_windows(jnp.dot(dqkv, wqkv.T, preferred_element_type=f32).reshape(nwin, seq, window_width), count)
    dxn, first_gain_gradient, first_norm_bias_gradient = norm_backward(dh1, xn1, inv1, g1)
    input_gradient_total = input_gradient_first + dxn
    return (final_output, input_gradient_total, (first_gain_gradient, first_norm_bias_gradient, query_key_value_gradient, query_value_bias_gradient, bias_table_gradient, projection_weight_gradient, projection_bias_gradient, second_gain_gradient, second_norm_bias_gradient, hidden_weight_gradient, hidden_bias_gradient, output_weight_gradient, output_bias_gradient))

def reference(block_input, ln1_gain, ln1_bias, qkv_weight, qv_bias, bias_table, proj_weight, proj_bias, ln2_gain, ln2_bias, fc1_weight, fc1_bias, fc2_weight, fc2_bias, region_ids, rel_index, cotangent):
    params = (ln1_gain, ln1_bias, qkv_weight, qv_bias, bias_table, proj_weight, proj_bias, ln2_gain, ln2_bias, fc1_weight, fc1_bias, fc2_weight, fc2_bias)
    block = IMG_DEV * N_SHARD
    steps_count = block_input.shape[0] // block
    xs = block_input.reshape((steps_count, block) + block_input.shape[1:])
    dys = cotangent.reshape((steps_count, block) + block_input.shape[1:])
    init = tuple((jnp.zeros(p.shape, jnp.float32) for p in params))

    def step(acc, item):
        final_output, input_gradient_total, grads = block_pass(item[0], item[1], params, rel_index, region_ids)
        return (tuple((a + g for a, g in zip(acc, grads))), (final_output, input_gradient_total))
    acc, outs = lax.scan(step, init, (xs, dys))
    return (outs[0].reshape(block_input.shape), outs[1].reshape(block_input.shape), acc[0], acc[1], acc[2], acc[3], acc[4], acc[5], acc[6], acc[7], acc[8], acc[9], acc[10], acc[11], acc[12])
```

```python
import functools

import jax
import jax.numpy as jnp
from jax import lax
from jax.experimental import pallas as pl
from jax.experimental.pallas import tpu as pltpu
from jax.sharding import PartitionSpec as P

SIDE = 14
WIN = 7
SHIFT = 3
TABLE = 169

EPS = 1e-05
MASKED = -100.0
INV_ROOT_TWO = 0.7071067811865476
INV_ROOT_TWO_PI = 0.3989422804014327

GRID = SIDE // WIN
NWIN = GRID * GRID
SEQ = WIN * WIN
PAD = 64
LANES = 128
ROWS = NWIN * PAD
SLOTS = 16
HIDDEN_TILE = 512
FAR = -1e30

f32 = jnp.float32
bf = jnp.bfloat16
NT = (((1,), (1,)), ((), ()))
TN = (((0,), (0,)), ((), ()))


def nn(a, b):
    return jnp.dot(a, b, preferred_element_type=f32)


def nt(a, b):
    return lax.dot_general(a, b, NT, preferred_element_type=f32)


def tn(a, b):
    return lax.dot_general(a, b, TN, preferred_element_type=f32)


def window_chunks():
    chunks = []
    for a in range(GRID):
        for b in range(GRID):
            for r in range(WIN):
                row = (WIN * a + r + SHIFT) % SIDE
                start = (WIN * b + SHIFT) % SIDE
                first = min(WIN, SIDE - start)
                at = r * WIN
                chunks.append((a * GRID + b, at, row, start, first))
                if first < WIN:
                    chunks.append((a * GRID + b, at + first, row, 0, WIN - first))
    return chunks


CHUNKS = window_chunks()


def gather_image(img, src, dst, first):
    for w, at, row, col, size in CHUNKS:
        dst[first + w, at : at + size, :] = src[img, row, col : col + size, :]


def scatter_image(img, src, first, dst):
    for w, at, row, col, size in CHUNKS:
        dst[img, row, col : col + size, :] = src[first + w, at : at + size, :]


def zero_pad_rows(dst, count):
    width = dst.shape[-1]
    for w in range(count):
        dst[w, SEQ:, :] = jnp.zeros((PAD - SEQ, width), dst.dtype)


def norm_rows(v):
    centered = v - jnp.mean(v, -1, keepdims=True)
    inv = lax.rsqrt(jnp.mean(centered * centered, -1, keepdims=True) + EPS)
    return centered * inv, inv


def norm_rows_backward(g, vn, inv, gain):
    dvn = g * gain
    return inv * (
        dvn
        - jnp.mean(dvn, -1, keepdims=True)
        - vn * jnp.mean(dvn * vn, -1, keepdims=True)
    )


def colsum(v):
    return jnp.sum(v, 0, keepdims=True)


def head_mask(hdim):
    shape = (LANES // hdim * PAD, LANES)
    rows = lax.broadcasted_iota(jnp.int32, shape, 0) // PAD
    lanes = lax.broadcasted_iota(jnp.int32, shape, 1) // hdim
    return (rows == lanes).astype(f32).astype(bf)


def segment_ones(n):
    rows = lax.broadcasted_iota(jnp.int32, (n, n), 0) // PAD
    lanes = lax.broadcasted_iota(jnp.int32, (n, n), 1) // PAD
    return (rows == lanes).astype(f32).astype(bf)


def spread(v, reps, mask):
    return jnp.concatenate([v] * reps, 0) * mask


def fold(v, reps, mask_f):
    out = None
    for h in range(reps):
        part = v[h * PAD : (h + 1) * PAD] * mask_f[h * PAD : h * PAD + 1, :]
        out = part if out is None else out + part
    return out


def load_halves(pairs, sems, index):
    copies = []
    for i, (own, other, full) in enumerate(pairs):
        n = own.shape[0]
        copies.append(pltpu.make_async_copy(own, full.at[pl.ds(index * n, n)], sems.at[2 * i]))
        copies.append(
            pltpu.make_async_copy(other, full.at[pl.ds((1 - index) * n, n)], sems.at[2 * i + 1])
        )
    for c in copies:
        c.start()
    return copies


def attention_forward(
    scal, x, wqkv_a, wqkv_b, wp_a, wp_b, vecs, extra,
    qkv_out, probs_out, o_out, x1_out,
    wqkv, wp, xw, hw, hmask, ones, sems, *, hdim,
):
    width = xw.shape[-1]
    reps = LANES // hdim
    groups = width // LANES
    scale = hdim ** (-0.5)

    @pl.when(pl.program_id(0) == 0)
    def _():
        copies = load_halves(((wqkv_a, wqkv_b, wqkv), (wp_a, wp_b, wp)), sems, scal[0])
        zero_pad_rows(xw, NWIN)
        hmask[...] = head_mask(hdim)
        ones[...] = segment_ones(reps * PAD)
        for c in copies:
            c.wait()

    gather_image(0, x, xw, 0)

    def norm_step(w, carry):
        vn, _ = norm_rows(xw[w])
        h = vn * vecs[0:1, :] + vecs[1:2, :]
        hw[pl.ds(w * PAD, PAD), :] = h.astype(bf)
        return carry

    lax.fori_loop(0, NWIN, norm_step, 0)
    part = nn(hw[...], wqkv[:, 0:width])
    qkv_out[:, 0:width] = ((part + vecs[2:3, :]) * scale).astype(bf)
    part = nn(hw[...], wqkv[:, width : 2 * width])
    qkv_out[:, width : 2 * width] = part.astype(bf)
    part = nn(hw[...], wqkv[:, 2 * width : 3 * width])
    qkv_out[:, 2 * width : 3 * width] = (part + vecs[3:4, :]).astype(bf)

    def attend(w, carry):
        rows = pl.ds(pl.multiple_of(w * PAD, PAD), PAD)
        for g in range(groups):
            lo = g * LANES
            q = qkv_out[rows, lo : lo + LANES]
            k = qkv_out[rows, width + lo : width + lo + LANES]
            v = qkv_out[rows, 2 * width + lo : 2 * width + lo + LANES]
            s = nt(q, spread(k, reps, hmask[...])) + extra[w, g]
            e = jnp.exp(s)
            total = nn(e.astype(bf), ones[...])
            p = (e / total).astype(bf)
            probs_out[w, g] = p
            o_out[rows, lo : lo + LANES] = nn(p, spread(v, reps, hmask[...])).astype(bf)
        return carry

    lax.fori_loop(0, NWIN, attend, 0)
    branch = nn(o_out[...], wp[...]) + vecs[4:5, :]
    x1_out[...] = xw[...].reshape(ROWS, width) + branch


def put(buf, half, slot, row, value):
    buf[half, slot, row : row + value.shape[0], :] = value


def feed_forward(
    scal, x1, dy, w1_a, w1_b, w2_a, w2_b, vecs, bias1,
    y_out, dx1_out, buf_a, buf_b, buf_c, small_out, bias1_out,
    w1, w2, dyw, dyb, h2, yacc, gacc, act, dub, sems,
):
    count = dy.shape[0]
    width = dyw.shape[-1]
    hidden = w1.shape[1]
    half_index = scal[0]
    labels = (scal[1], scal[2], scal[3])
    bufs = (buf_a, buf_b, buf_c)
    copies = load_halves(((w1_a, w1_b, w1), (w2_a, w2_b, w2)), sems, half_index)
    zero_pad_rows(dyw, count * NWIN)

    def gather_step(n, carry):
        gather_image(n, dy, dyw, n * NWIN)
        return carry

    lax.fori_loop(0, count, gather_step, 0)

    def norm_step(w, carry):
        rows = pl.ds(pl.multiple_of(w * PAD, PAD), PAD)
        v = x1[rows, :]
        vn, _ = norm_rows(v)
        h2[rows, :] = (vn * vecs[5:6, :] + vecs[6:7, :]).astype(bf)
        yacc[rows, :] = v + vecs[7:8, :]
        d = dyw[w]
        dyb[rows, :] = d.astype(bf)
        return carry + colsum(d)

    dysum = lax.fori_loop(0, count * NWIN, norm_step, jnp.zeros((1, width), f32))
    small_out[...] = jnp.zeros_like(small_out)
    small_out[0:1, :] = dysum
    for c in copies:
        c.wait()

    per_half = hidden // 2
    chunk2 = per_half // SLOTS
    chunk1 = width // 2 // SLOTS
    tiles = hidden // HIDDEN_TILE
    blocks = width // LANES
    for t in range(tiles):
        cols = slice(t * HIDDEN_TILE, (t + 1) * HIDDEN_TILE)

        def row_step(n, carry):
            rows = pl.ds(pl.multiple_of(n * ROWS, ROWS), ROWS)
            u = nn(h2[rows, :], w1[:, cols]) + bias1[t : t + 1, :]
            phi = 0.5 * (1.0 + lax.erf(u * INV_ROOT_TWO))
            act[rows, :] = (u * phi).astype(bf)
            slope = phi + u * jnp.exp(-0.5 * u * u) * INV_ROOT_TWO_PI
            du = nt(dyb[rows, :], w2[cols, :]) * slope
            dub[rows, :] = du.astype(bf)
            yacc[rows, :] = yacc[rows, :] + nn(act[rows, :], w2[cols, :])
            g = nt(dub[rows, :], w1[:, cols])
            if t == 0:
                gacc[rows, :] = g
            else:
                gacc[rows, :] = gacc[rows, :] + g
            return carry + colsum(du)

        bias1_out[t : t + 1, :] = lax.fori_loop(
            0, count, row_step, jnp.zeros((1, HIDDEN_TILE), f32)
        )
        dw2 = tn(act[...], dyb[...]).astype(bf)
        half = (t * HIDDEN_TILE) // per_half
        for i in range(HIDDEN_TILE // chunk2):
            c = (t * HIDDEN_TILE) % per_half // chunk2 + i
            for m in range(blocks):
                k = m * 2 // blocks
                at = (m - k * blocks // 2) * chunk2
                val = dw2[i * chunk2 : (i + 1) * chunk2, m * LANES : (m + 1) * LANES]
                put(bufs[k], half ^ half_index, c ^ labels[k], at, val)
        dw1 = tn(h2[...], dub[...]).astype(bf)
        k, base = W1_PLACE[t]
        for i in range(width // chunk1):
            half, c = i // SLOTS, i % SLOTS
            for m in range(HIDDEN_TILE // LANES):
                val = dw1[i * chunk1 : (i + 1) * chunk1, m * LANES : (m + 1) * LANES]
                put(bufs[k], half ^ half_index, c ^ labels[k], base + m * chunk1, val)

    def back_step(w, carry):
        gain_sum, bias_sum, dx_sum = carry
        rows = pl.ds(pl.multiple_of(w * PAD, PAD), PAD)
        vn, inv = norm_rows(x1[rows, :])
        g = gacc[rows, :]
        dx1 = dyw[w] + norm_rows_backward(g, vn, inv, vecs[5:6, :])
        dx1_out[rows, :] = dx1
        return gain_sum + colsum(g * vn), bias_sum + colsum(g), dx_sum + colsum(dx1)

    zero = jnp.zeros((1, width), f32)
    gain_sum, bias_sum, dx_sum = lax.fori_loop(0, count * NWIN, back_step, (zero, zero, zero))
    small_out[1:2, :] = gain_sum
    small_out[2:3, :] = bias_sum
    small_out[3:4, :] = dx_sum

    def scatter_step(n, carry):
        for w, at, row, col, size in CHUNKS:
            base = pl.multiple_of((n * NWIN + w) * PAD, PAD)
            y_out[n, row, col : col + size, :] = yacc[pl.ds(base, PAD), :][at : at + size, :]
        return carry

    lax.fori_loop(0, count, scatter_step, 0)


W1_PLACE = ((0, 128), (1, 128), (2, 0), (2, 64))
GROUP1_ROWS = (192, 192, 128)
GROUP2_ROWS = (80, 80, 96)


def attention_backward(
    scal, dx1, x, qkv, probs, o, wqkv_a, wqkv_b, wp_a, wp_b, vecs,
    dx_out, buf_a, buf_b, buf_c, small_out, dbias_out,
    wqkv, wp, xw, vns, hw, dwb, do, dqkv, dh, dxw, hmask, hmask_f, sems, *, hdim,
):
    width = xw.shape[-1]
    reps = LANES // hdim
    groups = width // LANES
    scale = hdim ** (-0.5)
    half_index = scal[0]
    labels = (scal[1], scal[2], scal[3])
    bufs = (buf_a, buf_b, buf_c)
    step = pl.program_id(0)
    base = pl.multiple_of(step * ROWS, ROWS)
    here = pl.ds(base, ROWS)

    @pl.when(step == 0)
    def _():
        copies = load_halves(((wqkv_a, wqkv_b, wqkv), (wp_a, wp_b, wp)), sems, half_index)
        zero_pad_rows(xw, NWIN)
        hmask[...] = head_mask(hdim)
        hmask_f[...] = hmask[...].astype(f32)
        small_out[...] = jnp.zeros_like(small_out)
        dbias_out[...] = jnp.zeros_like(dbias_out)
        for c in copies:
            c.wait()

    gather_image(0, x, xw, 0)

    def norm_step(w, carry):
        rows = pl.ds(pl.multiple_of(w * PAD, PAD), PAD)
        vn, _ = norm_rows(xw[w])
        h = vn * vecs[0:1, :] + vecs[1:2, :]
        hw[pl.ds(base + w * PAD, PAD), :] = h.astype(bf)
        dwb[pl.ds(base + w * PAD, PAD), :] = dx1[rows, :].astype(bf)
        return carry

    lax.fori_loop(0, NWIN, norm_step, 0)
    do[...] = nt(dwb[here, :], wp[...]).astype(bf)

    def attend(w, carry):
        qsum, vsum = carry
        rows = pl.ds(pl.multiple_of(w * PAD, PAD), PAD)
        orows = pl.ds(pl.multiple_of(base + w * PAD, PAD), PAD)
        qparts, vparts = [], []
        for g in range(groups):
            lo = g * LANES
            q = qkv[rows, lo : lo + LANES]
            k = qkv[rows, width + lo : width + lo + LANES]
            v = qkv[rows, 2 * width + lo : 2 * width + lo + LANES]
            pb = probs[w, g]
            d = do[rows, lo : lo + LANES]
            prod = d.astype(f32) * o[orows, lo : lo + LANES].astype(f32)
            left = jnp.concatenate([d, (-prod).astype(bf)], 1)
            right = jnp.concatenate([spread(v, reps, hmask[...]), hmask[...]], 1)
            ds = pb.astype(f32) * nt(left, right)
            dbias_out[g] = dbias_out[g] + ds
            dsb = ds.astype(bf)
            dq = nn(dsb, spread(k, reps, hmask[...])) * scale
            dk = fold(tn(dsb, q), reps, hmask_f)
            dv = fold(tn(pb, d), reps, hmask_f)
            qparts.append(colsum(dq))
            vparts.append(colsum(dv))
            dqkv[orows, lo : lo + LANES] = dq.astype(bf)
            dqkv[orows, width + lo : width + lo + LANES] = dk.astype(bf)
            dqkv[orows, 2 * width + lo : 2 * width + lo + LANES] = dv.astype(bf)
        return qsum + jnp.concatenate(qparts, 1), vsum + jnp.concatenate(vparts, 1)

    zero = jnp.zeros((1, width), f32)
    qsum, vsum = lax.fori_loop(0, NWIN, attend, (zero, zero))
    small_out[0:1, :] = small_out[0:1, :] + qsum
    small_out[1:2, :] = small_out[1:2, :] + vsum
    dh[...] = nt(dqkv[here, :], wqkv[...])

    def back_step(w, carry):
        gain_sum, bias_sum = carry
        rows = pl.ds(pl.multiple_of(w * PAD, PAD), PAD)
        vn, inv = norm_rows(xw[w])
        g = dh[rows, :]
        dxw[w] = dx1[rows, :] + norm_rows_backward(g, vn, inv, vecs[0:1, :])
        return gain_sum + colsum(g * vn), bias_sum + colsum(g)

    gain_sum, bias_sum = lax.fori_loop(0, NWIN, back_step, (zero, zero))
    small_out[2:3, :] = small_out[2:3, :] + gain_sum
    small_out[3:4, :] = small_out[3:4, :] + bias_sum
    scatter_image(0, dxw, 0, dx_out)

    @pl.when(step == pl.num_programs(0) - 1)
    def _():
        chunk = width // 2 // SLOTS
        blocks = width // LANES
        for part in range(3):
            dw = tn(hw[...], dqkv[:, part * width : (part + 1) * width]).astype(bf)
            for i in range(width // chunk):
                half, c = i // SLOTS, i % SLOTS
                for m in range(blocks):
                    val = dw[i * chunk : (i + 1) * chunk, m * LANES : (m + 1) * LANES]
                    put(bufs[part], half ^ half_index, c ^ labels[part], m * chunk, val)
        dw = tn(o[...], dwb[...]).astype(bf)
        for i in range(width // chunk):
            half, c = i // SLOTS, i % SLOTS
            for m in range(blocks):
                k = min(m, 2)
                at = blocks * chunk + (m - k) * chunk
                val = dw[i * chunk : (i + 1) * chunk, m * LANES : (m + 1) * LANES]
                put(bufs[k], half ^ half_index, c ^ labels[k], at, val)


def unpack(scal, a1, b1, c1, a2, b2, c2, w1, w2, wqkv, wp):
    c = pl.program_id(0)
    slots = tuple(c ^ scal[1 + k] for k in range(3))
    g1 = (a1, b1, c1)
    g2 = (a2, b2, c2)
    chunk1 = w1.shape[0]
    chunk2 = w2.shape[0]
    blocks = w2.shape[1] // LANES
    for m in range(blocks):
        k = m * 2 // blocks
        at = (m - k * blocks // 2) * chunk2
        w2[:, m * LANES : (m + 1) * LANES] = g1[k][slots[k], at : at + chunk2, :].astype(f32)
    for t, (k, base) in enumerate(W1_PLACE):
        for m in range(HIDDEN_TILE // LANES):
            lo = t * HIDDEN_TILE + m * LANES
            at = base + m * chunk1
            w1[:, lo : lo + LANES] = g1[k][slots[k], at : at + chunk1, :].astype(f32)
    for part in range(3):
        for m in range(blocks):
            lo = (part * blocks + m) * LANES
            at = m * chunk1
            wqkv[:, lo : lo + LANES] = g2[part][slots[part], at : at + chunk1, :].astype(f32)
    for m in range(blocks):
        k = min(m, 2)
        at = blocks * chunk1 + (m - k) * chunk1
        wp[:, m * LANES : (m + 1) * LANES] = g2[k][slots[k], at : at + chunk1, :].astype(f32)


def vmem():
    return pl.BlockSpec(memory_space=pltpu.VMEM)


def anywhere():
    return pl.BlockSpec(memory_space=pl.ANY)


def smem():
    return pl.BlockSpec(memory_space=pltpu.SMEM)


def params(limit=60 << 20):
    return pltpu.CompilerParams(vmem_limit_bytes=limit)


def cost(flops, size):
    return pl.CostEstimate(flops=flops, bytes_accessed=size, transcendentals=0)


def run_attention_forward(scal, x, wqkv, wp, vecs, extra, hdim):
    count, width = x.shape[0], x.shape[-1]
    rows = count * ROWS
    reps = LANES // hdim
    groups = width // LANES
    image = lambda n: (n, 0, 0, 0)
    return pl.pallas_call(
        functools.partial(attention_forward, hdim=hdim),
        grid=(count,),
        in_specs=[
            smem(),
            pl.BlockSpec((1, SIDE, SIDE, width), image),
            anywhere(), anywhere(), anywhere(), anywhere(),
            vmem(), vmem(),
        ],
        out_specs=[
            pl.BlockSpec((ROWS, 3 * width), lambda n: (n, 0)),
            pl.BlockSpec((NWIN, groups, PAD, reps * PAD), image),
            pl.BlockSpec((ROWS, width), lambda n: (n, 0)),
            pl.BlockSpec((ROWS, width), lambda n: (n, 0)),
        ],
        out_shape=[
            jax.ShapeDtypeStruct((rows, 3 * width), bf),
            jax.ShapeDtypeStruct((count * NWIN, groups, PAD, reps * PAD), bf),
            jax.ShapeDtypeStruct((rows, width), bf),
            jax.ShapeDtypeStruct((rows, width), f32),
        ],
        scratch_shapes=[
            pltpu.VMEM((width, 3 * width), bf),
            pltpu.VMEM((width, width), bf),
            pltpu.VMEM((NWIN, PAD, width), f32),
            pltpu.VMEM((ROWS, width), bf),
            pltpu.VMEM((reps * PAD, LANES), bf),
            pltpu.VMEM((reps * PAD, reps * PAD), bf),
            pltpu.SemaphoreType.DMA((4,)),
        ],
        compiler_params=params(),
        cost_estimate=cost(8 * rows * width * width, 12 << 20),
        name="attention_forward",
    )(scal, x, *wqkv, *wp, vecs, extra)


def run_feed_forward(scal, x1, dy, w1, w2, vecs, bias1):
    count, width = dy.shape[0], dy.shape[-1]
    rows = count * ROWS
    hidden = w1[0].shape[1]
    bufs = [jax.ShapeDtypeStruct((2, SLOTS, r, LANES), bf) for r in GROUP1_ROWS]
    return pl.pallas_call(
        feed_forward,
        in_specs=[smem(), vmem(), vmem(), anywhere(), anywhere(), anywhere(), anywhere(), vmem(), vmem()],
        out_specs=[vmem()] * 7,
        out_shape=[
            jax.ShapeDtypeStruct(dy.shape, f32),
            jax.ShapeDtypeStruct((rows, width), f32),
            *bufs,
            jax.ShapeDtypeStruct((8, width), f32),
            jax.ShapeDtypeStruct((hidden // HIDDEN_TILE, HIDDEN_TILE), f32),
        ],
        scratch_shapes=[
            pltpu.VMEM((width, hidden), bf),
            pltpu.VMEM((hidden, width), bf),
            pltpu.VMEM((count * NWIN, PAD, width), f32),
            pltpu.VMEM((rows, width), bf),
            pltpu.VMEM((rows, width), bf),
            pltpu.VMEM((rows, width), f32),
            pltpu.VMEM((rows, width), f32),
            pltpu.VMEM((rows, HIDDEN_TILE), bf),
            pltpu.VMEM((rows, HIDDEN_TILE), bf),
            pltpu.SemaphoreType.DMA((4,)),
        ],
        compiler_params=params(),
        cost_estimate=cost(12 * rows * width * hidden, 20 << 20),
        name="feed_forward",
    )(scal, x1, dy, *w1, *w2, vecs, bias1)


def run_attention_backward(scal, dx1, x, qkv, probs, o, wqkv, wp, vecs, hdim):
    count, width = x.shape[0], x.shape[-1]
    rows = count * ROWS
    reps = LANES // hdim
    groups = width // LANES
    image = lambda n: (n, 0, 0, 0)
    bufs = [jax.ShapeDtypeStruct((2, SLOTS, r, LANES), bf) for r in GROUP2_ROWS]
    return pl.pallas_call(
        functools.partial(attention_backward, hdim=hdim),
        grid=(count,),
        in_specs=[
            smem(),
            pl.BlockSpec((ROWS, width), lambda n: (n, 0)),
            pl.BlockSpec((1, SIDE, SIDE, width), image),
            pl.BlockSpec((ROWS, 3 * width), lambda n: (n, 0)),
            pl.BlockSpec((NWIN, groups, PAD, reps * PAD), image),
            vmem(),
            anywhere(), anywhere(), anywhere(), anywhere(),
            vmem(),
        ],
        out_specs=[pl.BlockSpec((1, SIDE, SIDE, width), image)] + [vmem()] * 5,
        out_shape=[
            jax.ShapeDtypeStruct(x.shape, f32),
            *bufs,
            jax.ShapeDtypeStruct((8, width), f32),
            jax.ShapeDtypeStruct((groups, PAD, reps * PAD), f32),
        ],
        scratch_shapes=[
            pltpu.VMEM((width, 3 * width), bf),
            pltpu.VMEM((width, width), bf),
            pltpu.VMEM((NWIN, PAD, width), f32),
            pltpu.VMEM((8, LANES), f32),
            pltpu.VMEM((rows, width), bf),
            pltpu.VMEM((rows, width), bf),
            pltpu.VMEM((ROWS, width), bf),
            pltpu.VMEM((rows, 3 * width), bf),
            pltpu.VMEM((ROWS, width), f32),
            pltpu.VMEM((NWIN, PAD, width), f32),
            pltpu.VMEM((reps * PAD, LANES), bf),
            pltpu.VMEM((reps * PAD, LANES), f32),
            pltpu.SemaphoreType.DMA((4,)),
        ],
        compiler_params=params(),
        cost_estimate=cost(16 * rows * width * width, 20 << 20),
        name="attention_backward",
    )(scal, dx1, x, qkv, probs, o, *wqkv, *wp, vecs)


def run_unpack(scal, bufs1, bufs2, shapes):
    def rows_of(shape):
        return pl.BlockSpec((shape[0] // SLOTS, shape[1]), lambda c: (c, 0))

    return pl.pallas_call(
        unpack,
        grid=(SLOTS,),
        in_specs=[smem()] + [vmem()] * 6,
        out_specs=[rows_of(s) for s in shapes],
        out_shape=[jax.ShapeDtypeStruct(s, f32) for s in shapes],
        compiler_params=params(),
        name="unpack",
    )(scal, *bufs1, *bufs2)


def padded_extra(table, rel_index, region_ids, groups, reps):
    short = PAD - SEQ
    rel = jnp.pad(rel_index, ((0, short), (0, short)), constant_values=-1).reshape(1, -1)
    onehot = rel == jnp.arange(TABLE, dtype=jnp.int32)[:, None]
    bias = lax.dot_general(table, onehot.astype(bf), TN, preferred_element_type=f32)
    bias = bias.reshape(groups, reps, PAD, PAD).transpose(0, 2, 1, 3)
    labels = region_ids.reshape(GRID, WIN, GRID, WIN).transpose(0, 2, 1, 3).reshape(NWIN, SEQ)
    same = labels[:, :, None] == labels[:, None, :]
    mask = jnp.where(same, f32(0.0), f32(MASKED))
    mask = jnp.pad(mask, ((0, 0), (0, short), (0, 0)))
    mask = jnp.pad(mask, ((0, 0), (0, 0), (0, short)), constant_values=FAR)
    extra = bias[None] + mask[:, None, :, None, :]
    return extra.reshape(NWIN, groups, PAD, reps * PAD), onehot


def pairs_of(axis_size, bit):
    return [(i, i ^ bit) for i in range(axis_size)]


def bit_orders(bits):
    if len(bits) < 3:
        return (bits,) * 3
    x, y, z = bits[0], bits[1], bits[2]
    rest = bits[3:]
    return ((x, y, z) + rest, (y, z, x) + rest, (z, x, y) + rest)


def slot_label(index, order):
    label = jnp.int32(0)
    for bit in order:
        label = 2 * label + (index // bit) % 2
    return label


def reduce_step(cur, bit, reps):
    half = cur.shape[0] // 2
    got = lax.ppermute(cur[half:], "rep", pairs_of(reps, bit))
    return cur[:half] + got


def per_device(
    block_input, ln1_gain, ln1_bias, qkv_weight, qv_bias, bias_table, proj_weight, proj_bias,
    ln2_gain, ln2_bias, fc1_weight, fc1_bias, fc2_weight, fc2_bias, region_ids, rel_index, cotangent,
):
    shards = lax.axis_size("shard")
    reps_axis = lax.axis_size("rep")
    width = block_input.shape[-1]
    heads = bias_table.shape[1] * shards
    hdim = width // heads
    reps = LANES // hdim
    groups = width // LANES
    fast = shards == 2 and reps_axis == SLOTS
    swap = [(0, 1), (1, 0)]
    shard_index = lax.axis_index("shard")
    rep_index = lax.axis_index("rep")

    vectors = (ln1_gain, ln1_bias, qv_bias[0], qv_bias[1], proj_bias, ln2_gain, ln2_bias, fc2_bias)
    own_vec = jnp.concatenate([jnp.stack(vectors), fc1_bias.reshape(-1, ln1_gain.shape[0])], 0)
    nvec = len(vectors)
    if fast:
        other_vec = lax.ppermute(own_vec, "shard", swap)
        other_table = lax.ppermute(bias_table, "shard", swap)
        low = shard_index == 0
        first = jnp.where(low, own_vec, other_vec)
        second = jnp.where(low, other_vec, own_vec)
        all_vec = jnp.stack([first, second])
        table = jnp.concatenate(
            [jnp.where(low, bias_table, other_table), jnp.where(low, other_table, bias_table)], 1
        )
        both = lambda w: (w, lax.ppermute(w, "shard", swap))
        orders = bit_orders(tuple(1 << i for i in range(SLOTS.bit_length() - 1)))
        labels = [slot_label(rep_index, order) for order in orders]
        scal = jnp.stack([shard_index.astype(jnp.int32)] + labels)
    else:
        all_vec = lax.all_gather(own_vec, "shard", axis=0)
        table = lax.all_gather(bias_table, "shard", axis=1, tiled=True)

        def both(w):
            full = lax.all_gather(w, "shard", axis=0, tiled=True)
            return jnp.split(full, 2, 0)

        scal = jnp.zeros((4,), jnp.int32)
    vecs = all_vec[:, :nvec].transpose(1, 0, 2).reshape(nvec, width).astype(f32)
    bias1 = all_vec[:, nvec:].reshape(-1, HIDDEN_TILE).astype(f32)
    wqkv = both(qkv_weight)
    wp = both(proj_weight)
    w1 = both(fc1_weight)
    w2 = both(fc2_weight)
    extra, onehot = padded_extra(table, rel_index, region_ids, groups, reps)

    qkv, probs, o, x1 = run_attention_forward(scal, block_input, wqkv, wp, vecs, extra, hdim)
    y, dx1, a1, b1, c1, small1, dbias1 = run_feed_forward(scal, x1, cotangent, w1, w2, vecs, bias1)
    dx, a2, b2, c2, small2, dbias = run_attention_backward(
        scal, dx1, block_input, qkv, probs, o, wqkv, wp, vecs, hdim
    )
    dbias = dbias.reshape(groups, PAD, reps, PAD).transpose(0, 2, 1, 3).reshape(heads, PAD * PAD)
    dtable = lax.dot_general(
        onehot.astype(f32), dbias, NT, precision=lax.Precision.HIGHEST
    )
    by_shard = lambda v: v.reshape(shards, -1)
    small_list = (
        (small2[2], ln1_gain.shape), (small2[3], ln1_bias.shape),
        (small1[3], proj_bias.shape), (small1[1], ln2_gain.shape), (small1[2], ln2_bias.shape),
        (dbias1.reshape(-1), fc1_bias.shape), (small1[0], fc2_bias.shape),
        (small2[0], ln1_gain.shape), (small2[1], ln1_bias.shape),
    )
    small = jnp.concatenate(
        [by_shard(v) for v, _ in small_list]
        + [dtable.reshape(TABLE, shards, -1).transpose(1, 0, 2).reshape(shards, -1)],
        1,
    ).astype(bf)
    shapes = [w.shape for w in (fc1_weight, fc2_weight, qkv_weight, proj_weight)]
    bufs = [a1, b1, c1, a2, b2, c2]
    if fast:
        short = -small.shape[1] % LANES
        small = jnp.pad(small, ((0, 0), (0, short))).reshape(2, -1, LANES)
        mine = lax.dynamic_index_in_dim(small, shard_index, 0, keepdims=False)
        theirs = lax.dynamic_index_in_dim(small, 1 - shard_index, 0, keepdims=False)
        total = mine + lax.ppermute(theirs, "shard", swap)
        for bit in orders[0]:
            total = total + lax.ppermute(total, "rep", pairs_of(reps_axis, bit))
        flat = total.reshape(-1).astype(f32)
        cur = [b[0] + lax.ppermute(b[1], "shard", swap) for b in bufs]
        steps = len(orders[0])
        for i in range(steps):
            cur = [reduce_step(v, orders[k % 3][i], reps_axis) for k, v in enumerate(cur)]
        for i in reversed(range(steps)):
            got = [
                lax.ppermute(v, "rep", pairs_of(reps_axis, orders[k % 3][i]))
                for k, v in enumerate(cur)
            ]
            cur = [jnp.concatenate([v, g], 0) for v, g in zip(cur, got)]
        gw1, gw2, gqkv, gp = run_unpack(scal, cur[:3], cur[3:], shapes)
    else:
        whole = [(2 * s[0] * shards // 2, s[1]) for s in shapes]
        halves = []
        for h in range(2):
            part = run_unpack(
                scal, [b[h] for b in bufs[:3]], [b[h] for b in bufs[3:]],
                [(s[0] // 2, s[1]) for s in whole],
            )
            halves.append(part)
        full = [jnp.concatenate([u, v], 0).astype(bf) for u, v in zip(*halves)]
        scattered = [lax.psum_scatter(v, "shard", scatter_dimension=0, tiled=True) for v in full]
        gw1, gw2, gqkv, gp = [lax.psum(v, "rep").astype(f32) for v in scattered]
        total = lax.psum(small, ("shard", "rep"))
        flat = lax.dynamic_index_in_dim(total, shard_index, 0, keepdims=False).astype(f32)
    parts = []
    offset = 0
    for _, shape in small_list:
        size = shape[0]
        parts.append(flat[offset : offset + size])
        offset += size
    gtable = flat[offset : offset + bias_table.size].reshape(bias_table.shape)
    gg1, gb1, gbp, gg2, gb2, gbf1, gbf2, gbq, gbv = parts
    return (
        y, dx, gg1, gb1, gqkv, jnp.stack([gbq, gbv]), gtable, gp, gbp, gg2, gb2, gw1, gbf1, gw2, gbf2,
    )


def solution(mesh):
    placed = (
        P(("shard", "rep"), None, None, None),
        P("shard"),
        P("shard"),
        P("shard", None),
        P(None, "shard"),
        P(None, "shard"),
        P("shard", None),
        P("shard"),
        P("shard"),
        P("shard"),
        P("shard", None),
        P("shard"),
        P("shard", None),
        P("shard"),
        P(),
        P(),
        P(("shard", "rep"), None, None, None),
    )
    return jax.shard_map(
        per_device,
        mesh=mesh,
        in_specs=placed,
        out_specs=(
            P(("shard", "rep"), None, None, None),
            P(("shard", "rep"), None, None, None),
            P("shard"),
            P("shard"),
            P("shard", None),
            P(None, "shard"),
            P(None, "shard"),
            P("shard", None),
            P("shard"),
            P("shard"),
            P("shard"),
            P("shard", None),
            P("shard"),
            P("shard", None),
            P("shard"),
        ),
        check_vma=False,
    )
```

```python
import functools

import jax
import jax.numpy as jnp
from jax import lax
from jax.experimental import pallas as pl
from jax.experimental.pallas import tpu as pltpu
from jax.sharding import PartitionSpec as P

SIDE = 14
WIN = 7
SHIFT = 3
TABLE = 169

EPS = 1e-05
MASKED = -100.0
INV_ROOT_TWO = 0.7071067811865476
INV_ROOT_TWO_PI = 0.3989422804014327

GRID = SIDE // WIN
NWIN = GRID * GRID
SEQ = WIN * WIN
PAD = 64
LANES = 128
ROWS = NWIN * PAD
SLOTS = 16
HIDDEN_TILE = 512
FAR = -1e30

f32 = jnp.float32
bf = jnp.bfloat16
NT = (((1,), (1,)), ((), ()))
TN = (((0,), (0,)), ((), ()))


def nn(a, b):
    return jnp.dot(a, b, preferred_element_type=f32)


def nt(a, b):
    return lax.dot_general(a, b, NT, preferred_element_type=f32)


def tn(a, b):
    return lax.dot_general(a, b, TN, preferred_element_type=f32)


def window_chunks():
    chunks = []
    for a in range(GRID):
        for b in range(GRID):
            for r in range(WIN):
                row = (WIN * a + r + SHIFT) % SIDE
                start = (WIN * b + SHIFT) % SIDE
                first = min(WIN, SIDE - start)
                at = r * WIN
                chunks.append((a * GRID + b, at, row, start, first))
                if first < WIN:
                    chunks.append((a * GRID + b, at + first, row, 0, WIN - first))
    return chunks


CHUNKS = window_chunks()


def gather_image(img, src, dst, first):
    for w, at, row, col, size in CHUNKS:
        dst[first + w, at : at + size, :] = src[img, row, col : col + size, :]


def scatter_image(img, src, first, dst):
    for w, at, row, col, size in CHUNKS:
        dst[img, row, col : col + size, :] = src[first + w, at : at + size, :]


def zero_pad_rows(dst, count):
    width = dst.shape[-1]
    for w in range(count):
        dst[w, SEQ:, :] = jnp.zeros((PAD - SEQ, width), dst.dtype)


def norm_rows(v):
    centered = v - jnp.mean(v, -1, keepdims=True)
    inv = lax.rsqrt(jnp.mean(centered * centered, -1, keepdims=True) + EPS)
    return centered * inv, inv


def norm_rows_backward(g, vn, inv, gain):
    dvn = g * gain
    return inv * (
        dvn
        - jnp.mean(dvn, -1, keepdims=True)
        - vn * jnp.mean(dvn * vn, -1, keepdims=True)
    )


def colsum(v):
    return jnp.sum(v, 0, keepdims=True)


def head_mask(hdim):
    shape = (LANES // hdim * PAD, LANES)
    rows = lax.broadcasted_iota(jnp.int32, shape, 0) // PAD
    lanes = lax.broadcasted_iota(jnp.int32, shape, 1) // hdim
    return (rows == lanes).astype(f32).astype(bf)


def segment_ones(n):
    rows = lax.broadcasted_iota(jnp.int32, (n, n), 0) // PAD
    lanes = lax.broadcasted_iota(jnp.int32, (n, n), 1) // PAD
    return (rows == lanes).astype(f32).astype(bf)


def spread(v, reps, mask):
    return jnp.concatenate([v] * reps, 0) * mask


def fold(v, reps, mask_f):
    out = None
    for h in range(reps):
        part = v[h * PAD : (h + 1) * PAD] * mask_f[h * PAD : h * PAD + 1, :]
        out = part if out is None else out + part
    return out


def load_halves(pairs, sems, index):
    copies = []
    for i, (own, other, full) in enumerate(pairs):
        n = own.shape[0]
        copies.append(pltpu.make_async_copy(own, full.at[pl.ds(index * n, n)], sems.at[2 * i]))
        copies.append(
            pltpu.make_async_copy(other, full.at[pl.ds((1 - index) * n, n)], sems.at[2 * i + 1])
        )
    for c in copies:
        c.start()
    return copies


def attention_forward(
    scal, x, wqkv_a, wqkv_b, wp_a, wp_b, vecs, extra,
    qkv_out, probs_out, o_out, x1_out,
    wqkv, wp, xw, hw, hmask, ones, sems, *, hdim,
):
    width = xw.shape[-1]
    reps = LANES // hdim
    groups = width // LANES
    scale = hdim ** (-0.5)

    @pl.when(pl.program_id(0) == 0)
    def _():
        copies = load_halves(((wqkv_a, wqkv_b, wqkv), (wp_a, wp_b, wp)), sems, scal[0])
        zero_pad_rows(xw, NWIN)
        hmask[...] = head_mask(hdim)
        ones[...] = segment_ones(reps * PAD)
        for c in copies:
            c.wait()

    gather_image(0, x, xw, 0)

    def norm_step(w, carry):
        vn, _ = norm_rows(xw[w])
        h = vn * vecs[0:1, :] + vecs[1:2, :]
        hw[pl.ds(w * PAD, PAD), :] = h.astype(bf)
        return carry

    lax.fori_loop(0, NWIN, norm_step, 0)
    part = nn(hw[...], wqkv[:, 0:width])
    qkv_out[:, 0:width] = ((part + vecs[2:3, :]) * scale).astype(bf)
    part = nn(hw[...], wqkv[:, width : 2 * width])
    qkv_out[:, width : 2 * width] = part.astype(bf)
    part = nn(hw[...], wqkv[:, 2 * width : 3 * width])
    qkv_out[:, 2 * width : 3 * width] = (part + vecs[3:4, :]).astype(bf)

    def attend(w, carry):
        rows = pl.ds(pl.multiple_of(w * PAD, PAD), PAD)
        for g in range(groups):
            lo = g * LANES
            q = qkv_out[rows, lo : lo + LANES]
            k = qkv_out[rows, width + lo : width + lo + LANES]
            v = qkv_out[rows, 2 * width + lo : 2 * width + lo + LANES]
            s = nt(q, spread(k, reps, hmask[...])) + extra[w, g]
            e = jnp.exp(s)
            total = nn(e.astype(bf), ones[...])
            p = (e / total).astype(bf)
            probs_out[w, g] = p
            o_out[rows, lo : lo + LANES] = nn(p, spread(v, reps, hmask[...])).astype(bf)
        return carry

    lax.fori_loop(0, NWIN, attend, 0)
    branch = nn(o_out[...], wp[...]) + vecs[4:5, :]
    x1_out[...] = xw[...].reshape(ROWS, width) + branch


def put(comm, color, half, slot, row, value):
    rows, start = color
    at = pl.multiple_of(start + slot * rows + row, 16)
    comm[half, pl.ds(at, value.shape[0]), :] = value


def color_table(rows):
    table = []
    start = 0
    for r in rows:
        table.append((r, start))
        start += SLOTS * r
    return table


def send_out(comm, keep_out, send_out_ref, sems):
    copies = [
        pltpu.make_async_copy(comm.at[0], keep_out, sems.at[0]),
        pltpu.make_async_copy(comm.at[1], send_out_ref, sems.at[1]),
    ]
    for c in copies:
        c.start()
    return copies


def feed_forward(
    scal, x1, dy, w1_a, w1_b, w2_a, w2_b, vecs, bias1,
    y_out, dx1_out, keep_out, send_out_ref, small_out, bias1_out,
    comm, w1, w2, dyw, dyb, h2, yacc, gacc, act, dub, sems,
):
    count = dy.shape[0]
    width = dyw.shape[-1]
    hidden = w1.shape[1]
    half_index = scal[0]
    labels = (scal[1], scal[2], scal[3])
    colors = color_table(GROUP1_ROWS)
    copies = load_halves(((w1_a, w1_b, w1), (w2_a, w2_b, w2)), sems, half_index)
    zero_pad_rows(dyw, count * NWIN)

    def gather_step(n, carry):
        gather_image(n, dy, dyw, n * NWIN)
        return carry

    lax.fori_loop(0, count, gather_step, 0)

    def norm_step(w, carry):
        rows = pl.ds(pl.multiple_of(w * PAD, PAD), PAD)
        v = x1[rows, :]
        vn, _ = norm_rows(v)
        h2[rows, :] = (vn * vecs[5:6, :] + vecs[6:7, :]).astype(bf)
        yacc[rows, :] = v + vecs[7:8, :]
        d = dyw[w]
        dyb[rows, :] = d.astype(bf)
        return carry + colsum(d)

    dysum = lax.fori_loop(0, count * NWIN, norm_step, jnp.zeros((1, width), f32))
    small_out[...] = jnp.zeros_like(small_out)
    small_out[0:1, :] = dysum
    for c in copies:
        c.wait()

    per_half = hidden // 2
    chunk2 = per_half // SLOTS
    chunk1 = width // 2 // SLOTS
    tiles = hidden // HIDDEN_TILE
    blocks = width // LANES
    for t in range(tiles):
        cols = slice(t * HIDDEN_TILE, (t + 1) * HIDDEN_TILE)

        def row_step(n, carry):
            rows = pl.ds(pl.multiple_of(n * ROWS, ROWS), ROWS)
            u = nn(h2[rows, :], w1[:, cols]) + bias1[t : t + 1, :]
            phi = 0.5 * (1.0 + lax.erf(u * INV_ROOT_TWO))
            act[rows, :] = (u * phi).astype(bf)
            slope = phi + u * jnp.exp(-0.5 * u * u) * INV_ROOT_TWO_PI
            du = nt(dyb[rows, :], w2[cols, :]) * slope
            dub[rows, :] = du.astype(bf)
            yacc[rows, :] = yacc[rows, :] + nn(act[rows, :], w2[cols, :])
            g = nt(dub[rows, :], w1[:, cols])
            if t == 0:
                gacc[rows, :] = g
            else:
                gacc[rows, :] = gacc[rows, :] + g
            return carry + colsum(du)

        bias1_out[t : t + 1, :] = lax.fori_loop(
            0, count, row_step, jnp.zeros((1, HIDDEN_TILE), f32)
        )
        dw2 = tn(act[...], dyb[...]).astype(bf)
        half = (t * HIDDEN_TILE) // per_half
        for i in range(HIDDEN_TILE // chunk2):
            c = (t * HIDDEN_TILE) % per_half // chunk2 + i
            for m in range(blocks):
                k = m * 2 // blocks
                at = (m - k * blocks // 2) * chunk2
                val = dw2[i * chunk2 : (i + 1) * chunk2, m * LANES : (m + 1) * LANES]
                put(comm, colors[k], half ^ half_index, c ^ labels[k], at, val)
        dw1 = tn(h2[...], dub[...]).astype(bf)
        k, base = W1_PLACE[t]
        for i in range(width // chunk1):
            half, c = i // SLOTS, i % SLOTS
            for m in range(HIDDEN_TILE // LANES):
                val = dw1[i * chunk1 : (i + 1) * chunk1, m * LANES : (m + 1) * LANES]
                put(comm, colors[k], half ^ half_index, c ^ labels[k], base + m * chunk1, val)
    copies = send_out(comm, keep_out, send_out_ref, sems)

    def back_step(w, carry):
        gain_sum, bias_sum, dx_sum = carry
        rows = pl.ds(pl.multiple_of(w * PAD, PAD), PAD)
        vn, inv = norm_rows(x1[rows, :])
        g = gacc[rows, :]
        dx1 = dyw[w] + norm_rows_backward(g, vn, inv, vecs[5:6, :])
        dx1_out[rows, :] = dx1
        return gain_sum + colsum(g * vn), bias_sum + colsum(g), dx_sum + colsum(dx1)

    zero = jnp.zeros((1, width), f32)
    gain_sum, bias_sum, dx_sum = lax.fori_loop(0, count * NWIN, back_step, (zero, zero, zero))
    small_out[1:2, :] = gain_sum
    small_out[2:3, :] = bias_sum
    small_out[3:4, :] = dx_sum

    def scatter_step(n, carry):
        for w, at, row, col, size in CHUNKS:
            base = pl.multiple_of((n * NWIN + w) * PAD, PAD)
            y_out[n, row, col : col + size, :] = yacc[pl.ds(base, PAD), :][at : at + size, :]
        return carry

    lax.fori_loop(0, count, scatter_step, 0)
    for c in copies:
        c.wait()


W1_PLACE = ((0, 128), (1, 128), (2, 0), (2, 64))
GROUP1_ROWS = (192, 192, 128)
GROUP2_ROWS = (80, 80, 96)


def attention_backward(
    scal, dx1, x, qkv, probs, o, wqkv_a, wqkv_b, wp_a, wp_b, vecs,
    dx_out, keep_out, send_out_ref, small_out, dbias_out,
    comm, wqkv, wp, xw, hw, dwb, do, dqkv, dh, dxw, hmask, hmask_f, sems, *, hdim,
):
    width = xw.shape[-1]
    reps = LANES // hdim
    groups = width // LANES
    scale = hdim ** (-0.5)
    half_index = scal[0]
    labels = (scal[1], scal[2], scal[3])
    colors = color_table(GROUP2_ROWS)
    step = pl.program_id(0)
    base = pl.multiple_of(step * ROWS, ROWS)
    here = pl.ds(base, ROWS)

    @pl.when(step == 0)
    def _():
        copies = load_halves(((wqkv_a, wqkv_b, wqkv), (wp_a, wp_b, wp)), sems, half_index)
        zero_pad_rows(xw, NWIN)
        hmask[...] = head_mask(hdim)
        hmask_f[...] = hmask[...].astype(f32)
        small_out[...] = jnp.zeros_like(small_out)
        dbias_out[...] = jnp.zeros_like(dbias_out)
        for c in copies:
            c.wait()

    gather_image(0, x, xw, 0)

    def norm_step(w, carry):
        rows = pl.ds(pl.multiple_of(w * PAD, PAD), PAD)
        vn, _ = norm_rows(xw[w])
        h = vn * vecs[0:1, :] + vecs[1:2, :]
        hw[pl.ds(base + w * PAD, PAD), :] = h.astype(bf)
        dwb[pl.ds(base + w * PAD, PAD), :] = dx1[rows, :].astype(bf)
        return carry

    lax.fori_loop(0, NWIN, norm_step, 0)
    do[...] = nt(dwb[here, :], wp[...]).astype(bf)

    def attend(w, carry):
        qsum, vsum = carry
        rows = pl.ds(pl.multiple_of(w * PAD, PAD), PAD)
        orows = pl.ds(pl.multiple_of(base + w * PAD, PAD), PAD)
        qparts, vparts = [], []
        for g in range(groups):
            lo = g * LANES
            q = qkv[rows, lo : lo + LANES]
            k = qkv[rows, width + lo : width + lo + LANES]
            v = qkv[rows, 2 * width + lo : 2 * width + lo + LANES]
            pb = probs[w, g]
            d = do[rows, lo : lo + LANES]
            prod = d.astype(f32) * o[orows, lo : lo + LANES].astype(f32)
            left = jnp.concatenate([d, (-prod).astype(bf)], 1)
            right = jnp.concatenate([spread(v, reps, hmask[...]), hmask[...]], 1)
            ds = pb.astype(f32) * nt(left, right)
            dbias_out[g] = dbias_out[g] + ds
            dsb = ds.astype(bf)
            dq = nn(dsb, spread(k, reps, hmask[...])) * scale
            dk = fold(tn(dsb, q), reps, hmask_f)
            dv = fold(tn(pb, d), reps, hmask_f)
            qparts.append(colsum(dq))
            vparts.append(colsum(dv))
            dqkv[orows, lo : lo + LANES] = dq.astype(bf)
            dqkv[orows, width + lo : width + lo + LANES] = dk.astype(bf)
            dqkv[orows, 2 * width + lo : 2 * width + lo + LANES] = dv.astype(bf)
        return qsum + jnp.concatenate(qparts, 1), vsum + jnp.concatenate(vparts, 1)

    zero = jnp.zeros((1, width), f32)
    qsum, vsum = lax.fori_loop(0, NWIN, attend, (zero, zero))
    small_out[0:1, :] = small_out[0:1, :] + qsum
    small_out[1:2, :] = small_out[1:2, :] + vsum
    dh[...] = nt(dqkv[here, :], wqkv[...])

    def back_step(w, carry):
        gain_sum, bias_sum = carry
        rows = pl.ds(pl.multiple_of(w * PAD, PAD), PAD)
        vn, inv = norm_rows(xw[w])
        g = dh[rows, :]
        dxw[w] = dx1[rows, :] + norm_rows_backward(g, vn, inv, vecs[0:1, :])
        return gain_sum + colsum(g * vn), bias_sum + colsum(g)

    gain_sum, bias_sum = lax.fori_loop(0, NWIN, back_step, (zero, zero))
    small_out[2:3, :] = small_out[2:3, :] + gain_sum
    small_out[3:4, :] = small_out[3:4, :] + bias_sum
    scatter_image(0, dxw, 0, dx_out)

    @pl.when(step == pl.num_programs(0) - 1)
    def _():
        chunk = width // 2 // SLOTS
        blocks = width // LANES
        for part in range(3):
            dw = tn(hw[...], dqkv[:, part * width : (part + 1) * width]).astype(bf)
            for i in range(width // chunk):
                half, c = i // SLOTS, i % SLOTS
                for m in range(blocks):
                    val = dw[i * chunk : (i + 1) * chunk, m * LANES : (m + 1) * LANES]
                    put(comm, colors[part], half ^ half_index, c ^ labels[part], m * chunk, val)
        dw = tn(o[...], dwb[...]).astype(bf)
        for i in range(width // chunk):
            half, c = i // SLOTS, i % SLOTS
            for m in range(blocks):
                k = min(m, 2)
                at = blocks * chunk + (m - k) * chunk
                val = dw[i * chunk : (i + 1) * chunk, m * LANES : (m + 1) * LANES]
                put(comm, colors[k], half ^ half_index, c ^ labels[k], at, val)
        for c in send_out(comm, keep_out, send_out_ref, sems):
            c.wait()


def unpack(scal, *refs):
    pieces, (w1, w2, wqkv, wp) = refs[:-4], refs[-4:]
    per = len(pieces) // 3
    span = SLOTS // per
    chunk1 = w1.shape[0] // UNPACK_CHUNKS
    chunk2 = w2.shape[0] // UNPACK_CHUNKS
    blocks = w2.shape[1] // LANES
    for j in range(UNPACK_CHUNKS):
        c = pl.program_id(0) * UNPACK_CHUNKS + j
        rows1 = slice(j * chunk1, (j + 1) * chunk1)
        rows2 = slice(j * chunk2, (j + 1) * chunk2)
        slots = tuple(c ^ scal[1 + k] for k in range(3))

        def copy_from(k, source, slot):
            def take(at, size):
                return source[slot, at : at + size, :].astype(f32)

            for m in range(blocks):
                if m * 2 // blocks == k:
                    at = (m - k * blocks // 2) * chunk2
                    w2[rows2, m * LANES : (m + 1) * LANES] = take(at, chunk2)
            for t, (kk, base) in enumerate(W1_PLACE):
                if kk == k:
                    for m in range(HIDDEN_TILE // LANES):
                        lo = t * HIDDEN_TILE + m * LANES
                        w1[rows1, lo : lo + LANES] = take(base + m * chunk1, chunk1)
            low = GROUP1_ROWS[k]
            for m in range(blocks):
                lo = (k * blocks + m) * LANES
                wqkv[rows1, lo : lo + LANES] = take(low + m * chunk1, chunk1)
            for m in range(blocks):
                if min(m, 2) == k:
                    at = low + blocks * chunk1 + (m - k) * chunk1
                    wp[rows1, m * LANES : (m + 1) * LANES] = take(at, chunk1)

        for k in range(3):
            if per == 1:
                copy_from(k, pieces[k], slots[k])
            else:
                for p in range(per):

                    @pl.when(slots[k] // span == p)
                    def _(k=k, p=p):
                        copy_from(k, pieces[k * per + p], slots[k] % span)


def combine(count, *refs):
    ins, outs = refs[: 2 * count], refs[2 * count :]
    groups = count // 3
    for k in range(3):
        keep, send = outs[2 * k], outs[2 * k + 1]
        half = keep.shape[0]
        at = 0
        for g in range(groups):
            a, b = ins[2 * (k * groups + g)], ins[2 * (k * groups + g) + 1]
            n = a.shape[1]
            keep[:, at : at + n, :] = a[:half] + b[:half]
            send[:, at : at + n, :] = a[half:] + b[half:]
            at += n


def run_combine(groups):
    count = sum(len(g) for g in groups)
    out_shape = []
    for g in groups:
        half = g[0][0].shape[0] // 2
        rows = sum(a.shape[1] for a, _ in g)
        out_shape += [jax.ShapeDtypeStruct((half, rows, LANES), bf)] * 2
    flat = [v for g in groups for pair in g for v in pair]
    size = 2 * sum(v.size for v in flat)
    outs = pl.pallas_call(
        functools.partial(combine, count),
        in_specs=[vmem()] * len(flat),
        out_specs=[vmem()] * len(out_shape),
        out_shape=out_shape,
        cost_estimate=cost(size // 4, 2 * size),
        compiler_params=params(),
        name="combine",
    )(*flat)
    return outs[0::2], outs[1::2]


def split_swap(rows, keep, got, *outs):
    for k, (r, start) in enumerate(color_table(rows)):
        half = SLOTS // 2
        stay, send = outs[2 * k], outs[2 * k + 1]
        for s in range(half):
            at = start + s * r
            far = start + (half + s) * r
            stay[s] = keep[at : at + r, :] + got[at : at + r, :]
            send[s] = keep[far : far + r, :] + got[far : far + r, :]


def run_split_swap(rows, keep, got):
    out_shape = [
        jax.ShapeDtypeStruct((SLOTS // 2, r, LANES), bf) for r in rows for _ in range(2)
    ]
    outs = pl.pallas_call(
        functools.partial(split_swap, rows),
        in_specs=[vmem()] * 2,
        out_specs=[vmem()] * len(out_shape),
        out_shape=out_shape,
        cost_estimate=cost(keep.size, 6 * keep.size),
        compiler_params=params(),
        name="split_swap",
    )(keep, got)
    return outs[0::2], outs[1::2]


UNPACK_CHUNKS = 4


def vmem():
    return pl.BlockSpec(memory_space=pltpu.VMEM)


def anywhere():
    return pl.BlockSpec(memory_space=pl.ANY)


def smem():
    return pl.BlockSpec(memory_space=pltpu.SMEM)


def params(limit=60 << 20):
    return pltpu.CompilerParams(vmem_limit_bytes=limit)


def cost(flops, size):
    return pl.CostEstimate(flops=flops, bytes_accessed=size, transcendentals=0)


def run_attention_forward(scal, x, wqkv, wp, vecs, extra, hdim):
    count, width = x.shape[0], x.shape[-1]
    rows = count * ROWS
    reps = LANES // hdim
    groups = width // LANES
    image = lambda n: (n, 0, 0, 0)
    return pl.pallas_call(
        functools.partial(attention_forward, hdim=hdim),
        grid=(count,),
        in_specs=[
            smem(),
            pl.BlockSpec((1, SIDE, SIDE, width), image),
            anywhere(), anywhere(), anywhere(), anywhere(),
            vmem(), vmem(),
        ],
        out_specs=[
            pl.BlockSpec((ROWS, 3 * width), lambda n: (n, 0)),
            pl.BlockSpec((NWIN, groups, PAD, reps * PAD), image),
            pl.BlockSpec((ROWS, width), lambda n: (n, 0)),
            pl.BlockSpec((ROWS, width), lambda n: (n, 0)),
        ],
        out_shape=[
            jax.ShapeDtypeStruct((rows, 3 * width), bf),
            jax.ShapeDtypeStruct((count * NWIN, groups, PAD, reps * PAD), bf),
            jax.ShapeDtypeStruct((rows, width), bf),
            jax.ShapeDtypeStruct((rows, width), f32),
        ],
        scratch_shapes=[
            pltpu.VMEM((width, 3 * width), bf),
            pltpu.VMEM((width, width), bf),
            pltpu.VMEM((NWIN, PAD, width), f32),
            pltpu.VMEM((ROWS, width), bf),
            pltpu.VMEM((reps * PAD, LANES), bf),
            pltpu.VMEM((reps * PAD, reps * PAD), bf),
            pltpu.SemaphoreType.DMA((4,)),
        ],
        compiler_params=params(),
        cost_estimate=cost(8 * rows * width * width, 12 << 20),
        name="attention_forward",
    )(scal, x, *wqkv, *wp, vecs, extra)


def run_feed_forward(scal, x1, dy, w1, w2, vecs, bias1):
    count, width = dy.shape[0], dy.shape[-1]
    rows = count * ROWS
    hidden = w1[0].shape[1]
    comm = (2, SLOTS * sum(GROUP1_ROWS), LANES)
    return pl.pallas_call(
        feed_forward,
        in_specs=[smem(), vmem(), vmem(), anywhere(), anywhere(), anywhere(), anywhere(), vmem(), vmem()],
        out_specs=[vmem(), vmem(), anywhere(), anywhere(), vmem(), vmem()],
        out_shape=[
            jax.ShapeDtypeStruct(dy.shape, f32),
            jax.ShapeDtypeStruct((rows, width), f32),
            jax.ShapeDtypeStruct(comm[1:], bf),
            jax.ShapeDtypeStruct(comm[1:], bf),
            jax.ShapeDtypeStruct((8, width), f32),
            jax.ShapeDtypeStruct((hidden // HIDDEN_TILE, HIDDEN_TILE), f32),
        ],
        scratch_shapes=[
            pltpu.VMEM(comm, bf),
            pltpu.VMEM((width, hidden), bf),
            pltpu.VMEM((hidden, width), bf),
            pltpu.VMEM((count * NWIN, PAD, width), f32),
            pltpu.VMEM((rows, width), bf),
            pltpu.VMEM((rows, width), bf),
            pltpu.VMEM((rows, width), f32),
            pltpu.VMEM((rows, width), f32),
            pltpu.VMEM((rows, HIDDEN_TILE), bf),
            pltpu.VMEM((rows, HIDDEN_TILE), bf),
            pltpu.SemaphoreType.DMA((4,)),
        ],
        compiler_params=params(),
        cost_estimate=cost(12 * rows * width * hidden, 20 << 20),
        name="feed_forward",
    )(scal, x1, dy, *w1, *w2, vecs, bias1)


def run_attention_backward(scal, dx1, x, qkv, probs, o, wqkv, wp, vecs, hdim):
    count, width = x.shape[0], x.shape[-1]
    rows = count * ROWS
    reps = LANES // hdim
    groups = width // LANES
    image = lambda n: (n, 0, 0, 0)
    comm = (2, SLOTS * sum(GROUP2_ROWS), LANES)
    return pl.pallas_call(
        functools.partial(attention_backward, hdim=hdim),
        grid=(count,),
        in_specs=[
            smem(),
            pl.BlockSpec((ROWS, width), lambda n: (n, 0)),
            pl.BlockSpec((1, SIDE, SIDE, width), image),
            pl.BlockSpec((ROWS, 3 * width), lambda n: (n, 0)),
            pl.BlockSpec((NWIN, groups, PAD, reps * PAD), image),
            vmem(),
            anywhere(), anywhere(), anywhere(), anywhere(),
            vmem(),
        ],
        out_specs=[
            pl.BlockSpec((1, SIDE, SIDE, width), image), anywhere(), anywhere(), vmem(), vmem(),
        ],
        out_shape=[
            jax.ShapeDtypeStruct(x.shape, f32),
            jax.ShapeDtypeStruct(comm[1:], bf),
            jax.ShapeDtypeStruct(comm[1:], bf),
            jax.ShapeDtypeStruct((8, width), f32),
            jax.ShapeDtypeStruct((groups, PAD, reps * PAD), f32),
        ],
        scratch_shapes=[
            pltpu.VMEM(comm, bf),
            pltpu.VMEM((width, 3 * width), bf),
            pltpu.VMEM((width, width), bf),
            pltpu.VMEM((NWIN, PAD, width), f32),
            pltpu.VMEM((rows, width), bf),
            pltpu.VMEM((rows, width), bf),
            pltpu.VMEM((ROWS, width), bf),
            pltpu.VMEM((rows, 3 * width), bf),
            pltpu.VMEM((ROWS, width), f32),
            pltpu.VMEM((NWIN, PAD, width), f32),
            pltpu.VMEM((reps * PAD, LANES), bf),
            pltpu.VMEM((reps * PAD, LANES), f32),
            pltpu.SemaphoreType.DMA((4,)),
        ],
        compiler_params=params(),
        cost_estimate=cost(16 * rows * width * width, 20 << 20),
        name="attention_backward",
    )(scal, dx1, x, qkv, probs, o, *wqkv, *wp, vecs)


def run_unpack(scal, pieces, shapes):
    def rows_of(shape):
        return pl.BlockSpec((shape[0] * UNPACK_CHUNKS // SLOTS, shape[1]), lambda c: (c, 0))

    return pl.pallas_call(
        unpack,
        grid=(SLOTS // UNPACK_CHUNKS,),
        in_specs=[smem()] + [vmem()] * len(pieces),
        out_specs=[rows_of(s) for s in shapes],
        out_shape=[jax.ShapeDtypeStruct(s, f32) for s in shapes],
        compiler_params=params(),
        name="unpack",
    )(scal, *pieces)


def padded_extra(table, rel_index, region_ids, groups, reps):
    short = PAD - SEQ
    rel = jnp.pad(rel_index, ((0, short), (0, short)), constant_values=-1).reshape(1, -1)
    onehot = rel == jnp.arange(TABLE, dtype=jnp.int32)[:, None]
    bias = lax.dot_general(table, onehot.astype(bf), TN, preferred_element_type=f32)
    bias = bias.reshape(groups, reps, PAD, PAD).transpose(0, 2, 1, 3)
    labels = region_ids.reshape(GRID, WIN, GRID, WIN).transpose(0, 2, 1, 3).reshape(NWIN, SEQ)
    same = labels[:, :, None] == labels[:, None, :]
    mask = jnp.where(same, f32(0.0), f32(MASKED))
    mask = jnp.pad(mask, ((0, 0), (0, short), (0, 0)))
    mask = jnp.pad(mask, ((0, 0), (0, 0), (0, short)), constant_values=FAR)
    extra = bias[None] + mask[:, None, :, None, :]
    return extra.reshape(NWIN, groups, PAD, reps * PAD), onehot


def pairs_of(axis_size, bit):
    return [(i, i ^ bit) for i in range(axis_size)]


def bit_orders(bits):
    if len(bits) < 3:
        return (bits,) * 3
    x, y, z = bits[0], bits[1], bits[2]
    rest = bits[3:]
    return ((x, y, z) + rest, (y, z, x) + rest, (z, x, y) + rest)


def slot_label(index, order):
    label = jnp.int32(0)
    for bit in order:
        label = 2 * label + (index // bit) % 2
    return label


def per_device(
    block_input, ln1_gain, ln1_bias, qkv_weight, qv_bias, bias_table, proj_weight, proj_bias,
    ln2_gain, ln2_bias, fc1_weight, fc1_bias, fc2_weight, fc2_bias, region_ids, rel_index, cotangent,
):
    shards = lax.axis_size("shard")
    reps_axis = lax.axis_size("rep")
    width = block_input.shape[-1]
    heads = bias_table.shape[1] * shards
    hdim = width // heads
    reps = LANES // hdim
    groups = width // LANES
    fast = shards == 2 and reps_axis == SLOTS
    swap = [(0, 1), (1, 0)]
    shard_index = lax.axis_index("shard")
    rep_index = lax.axis_index("rep")

    vectors = (ln1_gain, ln1_bias, qv_bias[0], qv_bias[1], proj_bias, ln2_gain, ln2_bias, fc2_bias)
    nvec = len(vectors)
    own_vec = jnp.concatenate(
        [ln1_gain, ln1_bias, qv_bias.reshape(-1), proj_bias, ln2_gain, ln2_bias, fc2_bias, fc1_bias]
    ).reshape(-1, ln1_gain.shape[0])
    if fast:
        other_vec = lax.ppermute(own_vec, "shard", swap)
        other_table = lax.ppermute(bias_table, "shard", swap)
        low = shard_index == 0
        first = jnp.where(low, own_vec, other_vec)
        second = jnp.where(low, other_vec, own_vec)
        all_vec = jnp.stack([first, second])
        table = jnp.concatenate(
            [jnp.where(low, bias_table, other_table), jnp.where(low, other_table, bias_table)], 1
        )
        both = lambda w: (w, lax.ppermute(w, "shard", swap))
        orders = bit_orders(tuple(1 << i for i in range(SLOTS.bit_length() - 1)))
        labels = [slot_label(rep_index, order) for order in orders]
        scal = jnp.stack([shard_index.astype(jnp.int32)] + labels)
    else:
        all_vec = lax.all_gather(own_vec, "shard", axis=0)
        table = lax.all_gather(bias_table, "shard", axis=1, tiled=True)

        def both(w):
            full = lax.all_gather(w, "shard", axis=0, tiled=True)
            return jnp.split(full, 2, 0)

        scal = jnp.zeros((4,), jnp.int32)
    vecs = all_vec[:, :nvec].transpose(1, 0, 2).reshape(nvec, width).astype(f32)
    bias1 = all_vec[:, nvec:].reshape(-1, HIDDEN_TILE).astype(f32)
    wqkv = both(qkv_weight)
    wp = both(proj_weight)
    w1 = both(fc1_weight)
    w2 = both(fc2_weight)
    extra, onehot = padded_extra(table, rel_index, region_ids, groups, reps)

    qkv, probs, o, x1 = run_attention_forward(scal, block_input, wqkv, wp, vecs, extra, hdim)
    y, dx1, keep1, send1, small1, dbias1 = run_feed_forward(
        scal, x1, cotangent, w1, w2, vecs, bias1
    )
    if fast:
        to_rep = lambda v, bit: lax.ppermute(v, "rep", pairs_of(reps_axis, bit))
        got1 = lax.ppermute(send1, "shard", swap)
        stay1, out1 = run_split_swap(GROUP1_ROWS, keep1, got1)
        dx1, out1 = lax.optimization_barrier((dx1, out1))
        back1 = [to_rep(v, orders[k][0]) for k, v in enumerate(out1)]
    dx, keep2, send2, small2, dbias = run_attention_backward(
        scal, dx1, block_input, qkv, probs, o, wqkv, wp, vecs, hdim
    )
    dbias = dbias.reshape(groups, PAD, reps, PAD).transpose(0, 2, 1, 3).reshape(heads, PAD * PAD)
    dtable = lax.dot_general(
        onehot.astype(f32), dbias, NT, precision=lax.Precision.HIGHEST
    )
    by_shard = lambda v: v.reshape(shards, -1)
    small_list = (
        (small2[2], ln1_gain.shape), (small2[3], ln1_bias.shape),
        (small1[3], proj_bias.shape), (small1[1], ln2_gain.shape), (small1[2], ln2_bias.shape),
        (dbias1.reshape(-1), fc1_bias.shape), (small1[0], fc2_bias.shape),
        (small2[0], ln1_gain.shape), (small2[1], ln1_bias.shape),
    )
    small = jnp.concatenate(
        [by_shard(v) for v, _ in small_list]
        + [dtable.reshape(TABLE, shards, -1).transpose(1, 0, 2).reshape(shards, -1)],
        1,
    ).astype(bf)
    shapes = [w.shape for w in (fc1_weight, fc2_weight, qkv_weight, proj_weight)]
    if fast:
        short = -small.shape[1] % LANES
        small = jnp.pad(small, ((0, 0), (0, short))).reshape(2, -1, LANES)
        mine = lax.dynamic_index_in_dim(small, shard_index, 0, keepdims=False)
        theirs = lax.dynamic_index_in_dim(small, 1 - shard_index, 0, keepdims=False)
        total = mine + lax.ppermute(theirs, "shard", swap)
        for bit in orders[0]:
            total = total + lax.ppermute(total, "rep", pairs_of(reps_axis, bit))
        flat = total.reshape(-1).astype(f32)
        got2 = lax.ppermute(send2, "shard", swap)
        stay2, out2 = run_split_swap(GROUP2_ROWS, keep2, got2)
        back2 = [to_rep(v, orders[k][0]) for k, v in enumerate(out2)]
        stay, out = run_combine(
            [[(stay1[k], back1[k]), (stay2[k], back2[k])] for k in range(3)]
        )
        steps = len(orders[0])
        for i in range(1, steps):
            back = [to_rep(v, orders[k][i]) for k, v in enumerate(out)]
            if i < steps - 1:
                stay, out = run_combine([[(stay[k], back[k])] for k in range(3)])
            else:
                cur = [a + b for a, b in zip(stay, back)]
        for i in reversed(range(steps)):
            got = [to_rep(v, orders[k][i]) for k, v in enumerate(cur)]
            if i:
                cur = [jnp.concatenate([v, g], 0) for v, g in zip(cur, got)]
        pieces = [v for pair in zip(cur, got) for v in pair]
        gw1, gw2, gqkv, gp = run_unpack(scal, pieces, shapes)
    else:
        whole = [(s[0] * shards // 2, s[1]) for s in shapes]
        halves = []
        for one, two in ((keep1, keep2), (send1, send2)):
            pieces = []
            for (r1, s1), (r2, s2) in zip(color_table(GROUP1_ROWS), color_table(GROUP2_ROWS)):
                p1 = one[s1 : s1 + SLOTS * r1].reshape(SLOTS, r1, LANES)
                p2 = two[s2 : s2 + SLOTS * r2].reshape(SLOTS, r2, LANES)
                pieces.append(jnp.concatenate([p1, p2], 1))
            halves.append(run_unpack(scal, pieces, whole))
        full = [jnp.concatenate([u, v], 0).astype(bf) for u, v in zip(*halves)]
        scattered = [lax.psum_scatter(v, "shard", scatter_dimension=0, tiled=True) for v in full]
        gw1, gw2, gqkv, gp = [lax.psum(v, "rep").astype(f32) for v in scattered]
        total = lax.psum(small, ("shard", "rep"))
        flat = lax.dynamic_index_in_dim(total, shard_index, 0, keepdims=False).astype(f32)
    parts = []
    offset = 0
    for _, shape in small_list:
        size = shape[0]
        parts.append(flat[offset : offset + size])
        offset += size
    gtable = flat[offset : offset + bias_table.size].reshape(bias_table.shape)
    gg1, gb1, gbp, gg2, gb2, gbf1, gbf2, gbq, gbv = parts
    return (
        y, dx, gg1, gb1, gqkv, jnp.stack([gbq, gbv]), gtable, gp, gbp, gg2, gb2, gw1, gbf1, gw2, gbf2,
    )


def solution(mesh):
    placed = (
        P(("shard", "rep"), None, None, None),
        P("shard"),
        P("shard"),
        P("shard", None),
        P(None, "shard"),
        P(None, "shard"),
        P("shard", None),
        P("shard"),
        P("shard"),
        P("shard"),
        P("shard", None),
        P("shard"),
        P("shard", None),
        P("shard"),
        P(),
        P(),
        P(("shard", "rep"), None, None, None),
    )
    return jax.shard_map(
        per_device,
        mesh=mesh,
        in_specs=placed,
        out_specs=(
            P(("shard", "rep"), None, None, None),
            P(("shard", "rep"), None, None, None),
            P("shard"),
            P("shard"),
            P("shard", None),
            P(None, "shard"),
            P(None, "shard"),
            P("shard", None),
            P("shard"),
            P("shard"),
            P("shard"),
            P("shard", None),
            P("shard"),
            P("shard", None),
            P("shard"),
        ),
        check_vma=False,
    )
```
